768 devices in a mesh: rows: 96 (over y, z), cols: 8 (over x, core).
Axes of the slice: x: 4, y: 8, z: 12, core: 2. Of those that a mesh axis runs over, the one named last changes fastest.
Arguments:
- users: bfloat16 [196608, 256], P('rows'), may hold values from -0.3984375 to 0.3984375
- items: bfloat16 [8, 1536, 256], P('cols'), may hold values from -6 to 6
- ratings: bfloat16 [96, 8, 64, 128, 128], P('rows', 'cols'), may hold values from -6 to 6
- tile_users: int32 [96, 8, 64], P('rows', 'cols'), may hold values from 0 to 15
- tile_items: int32 [96, 8, 64], P('rows', 'cols'), may hold values from 0 to 11
- tile_count: int32 [96, 8], P('rows', 'cols'), may hold values from 16 to 64, as said below
- send_list: int32 [96, 8, 8, 1], P('rows', 'cols'), may hold values from 0 to 11
- block_target: int32 [96, 8, 8], P('rows', 'cols'), may hold values from 0 to 11
- similarity: bfloat16 [96, 8, 8, 128, 128], P('rows', 'cols'), may hold values from -6 to 6
Outputs:
- new_items: float32 [8, 1536, 256], P('cols', 'rows')
The draws below stay inside these ranges and needn't reach their ends.
Inputs may be any that keep to these rules, and one draw needn't show every extreme that they name: `tile_count`: every draw has some device with all 64 slots live; the device differs from draw to draw.
All inputs are finite; a program needn't handle non-finite values.
Results may differ from the reference program's by a relative error of at most 0.00065.
Values may be sent and summed in bfloat16 or wider, within the bound.
A program may use at most 32 MiB of HBM per device.

```python
import jax
import jax.numpy as jnp
from jax import lax

R = 256
TILE = 128
UT_ROW = 16
TILES_DEV = 64
SLOTS = 1
GB = 8
IC = 1536
ICT = 12
NU = 196608
N_ROWS = 96
N_COLS = 8


def draw_tile_count(key, part):
    first, second, third = jax.random.split(key, 3)
    counts = jax.random.randint(first, (N_ROWS, N_COLS), TILES_DEV // 4, TILES_DEV + 1)
    row_pick = jax.random.randint(second, (), 0, N_ROWS)
    col_pick = jax.random.randint(third, (), 0, N_COLS)
    return counts.at[row_pick, col_pick].set(TILES_DEV).astype(jnp.int32)


def place_ends(result, rng, least, top_value):
    spot = [jax.random.randint(jax.random.fold_in(rng, axis), (), 0, length) for axis, length in enumerate(result.shape)]
    longest = result.shape.index(max(result.shape))
    neighbour = spot[:longest] + [(spot[longest] + 1) % result.shape[longest]] + spot[longest + 1:]
    return result.at[tuple(spot)].set(least).at[tuple(neighbour)].set(top_value)


def block_levels(key, extent, cuts, least, largest):
    gain = 1.0
    for axis_at, blocks in cuts:
        steps = jax.random.uniform(jax.random.fold_in(jax.random.fold_in(key, 6), axis_at), (blocks,), jnp.float32, least / len(cuts), largest / len(cuts))
        gain = gain * jnp.repeat(jnp.exp(steps), extent[axis_at] // blocks).reshape((-1,) + (1,) * (len(extent) - 1 - axis_at))
    return gain


def normal_values(own_key, dims, spread, limit, pieces=(), kind=jnp.bfloat16):
    result = spread * jax.random.normal(own_key, dims, jnp.float32)
    if pieces:
        result = result * block_levels(own_key, dims, pieces, -0.22, 0.18)
    return jnp.clip(result, -limit, limit).astype(kind)


def setup_inputs(seed: int = 0) -> dict:
    key_list = jax.random.split(jax.random.key(seed), 10)
    users = normal_values(key_list[0], (NU, R), 0.0625, 0.3984375, ((0, 96),))
    items = normal_values(key_list[1], (N_COLS, IC, R), 1.0, 6.0, ((0, 8),))
    ratings = normal_values(key_list[2], (N_ROWS, N_COLS, TILES_DEV, TILE, TILE), 1.0, 6.0, ((0, 96), (1, 8)))
    tile_users = place_ends(jax.random.randint(key_list[3], (N_ROWS, N_COLS, TILES_DEV), 0, UT_ROW), jax.random.fold_in(key_list[3], 1), 0, UT_ROW - 1).astype(jnp.int32)
    tile_items = place_ends(jax.random.randint(key_list[4], (N_ROWS, N_COLS, TILES_DEV), 0, ICT), jax.random.fold_in(key_list[4], 1), 0, ICT - 1).astype(jnp.int32)
    tile_count = draw_tile_count(jax.random.fold_in(key_list[9], 71), 0)
    send_list = place_ends(jax.random.randint(key_list[6], (N_ROWS, N_COLS, N_COLS, SLOTS), 0, ICT), jax.random.fold_in(key_list[6], 1), 0, ICT - 1).astype(jnp.int32)
    block_target = place_ends(jax.random.randint(key_list[7], (N_ROWS, N_COLS, GB), 0, ICT), jax.random.fold_in(key_list[7], 1), 0, ICT - 1).astype(jnp.int32)
    similarity = normal_values(key_list[8], (N_ROWS, N_COLS, GB, TILE, TILE), 1.0, 6.0, ((0, 96), (1, 8)))
    return {"users": users, "items": items, "ratings": ratings, "tile_users": tile_users, "tile_items": tile_items, "tile_count": tile_count, "send_list": send_list, "block_target": block_target, "similarity": similarity}


def reference(users, items, ratings, tile_users, tile_items, tile_count, send_list, block_target, similarity):
    ncols, icount, rank = items.shape
    tile = ratings.shape[-1]
    ntiles = icount // tile
    tiles_here = ratings.shape[2]
    slots = send_list.shape[-1]
    blocks = similarity.shape[2]
    user_tiles = users.reshape(N_ROWS, -1, tile, rank)
    item_tiles = items.reshape(ncols, ntiles, tile, rank)
    places = jnp.arange(tiles_here, dtype=jnp.int32)
    block_ids = jnp.arange(blocks, dtype=jnp.int32)
    sources = block_ids // slots
    slot_ids = block_ids % slots

    def device_step(index, grad):
        row = (index // ncols).astype(jnp.int32)
        col = (index % ncols).astype(jnp.int32)
        own_users = user_tiles[row]
        own_items = item_tiles[col]
        left = own_users[tile_users[row, col]].astype(jnp.float32)
        right = own_items[tile_items[row, col]].astype(jnp.float32)
        pred = jnp.einsum('tar,tbr->tab', left, right)
        live = (places < tile_count[row, col]).astype(jnp.float32)
        err = ((pred - ratings[row, col].astype(jnp.float32)) * live[:, None, None]).astype(jnp.bfloat16)
        part = jnp.einsum('tab,tar->tbr', err.astype(jnp.float32), left)
        local = jnp.zeros((ntiles, tile, rank), jnp.float32).at[tile_items[row, col]].add(part)
        picked = send_list[row, sources, col, slot_ids]
        panels = item_tiles[sources, picked].astype(jnp.float32)
        contrib = jnp.einsum('kab,kbr->kar', similarity[row, col].astype(jnp.float32), panels)
        local = local.at[block_target[row, col]].add(contrib)
        return grad.at[col].add(local)
    grad = lax.fori_loop(0, N_ROWS * ncols, device_step, jnp.zeros((ncols, ntiles, tile, rank), jnp.float32))
    grad = grad.reshape(ncols, icount, rank)
    meansq = jnp.mean(grad * grad)
    return items.astype(jnp.float32) - 0.5 * grad / jnp.sqrt(meansq + 1e-06)
```

```python
import functools

import jax
import jax.numpy as jnp
from jax import lax
from jax.experimental import pallas as pl
from jax.experimental.pallas import tpu as pltpu
from jax.sharding import PartitionSpec as P

NZ = 12
UNROLL = 4
MESH = pl.DeviceIdType.MESH
VMEM = pltpu.VMEM
F32 = jnp.float32
BF16 = jnp.bfloat16


def tiles_kernel(tu, ti, cnt, users, items, ratings, grad):
    grad[...] = jnp.zeros_like(grad)
    count = cnt[0]

    def step(g, carry):
        for u in range(UNROLL):
            t = g * UNROLL + u
            i = ti[t]
            left = users[tu[t]]
            pred = lax.dot_general(
                left, items[i], (((1,), (1,)), ((), ())), preferred_element_type=F32
            )
            err = jnp.where(t < count, pred - ratings[t].astype(F32), 0.0).astype(BF16)
            part = lax.dot_general(
                err, left, (((0,), (0,)), ((), ())), preferred_element_type=F32
            )
            grad[i] += part
        return carry

    lax.fori_loop(0, (count + UNROLL - 1) // UNROLL, step, 0)


def graph_kernel(blocks, target, similarity, incoming, grad_in, grad):
    grad[...] = grad_in[...]
    for k in range(blocks):
        grad[target[k]] += jnp.dot(
            similarity[k], incoming[k], preferred_element_type=F32
        )


def reduce_kernel(
    ny, nz, nc, grad, items, out,
    send_a, send_b, recv_a, recv_b, acc_a, acc_b, recv2_a, recv2_b,
    sq, recv_z, recv_y, recv_c, mine,
    ssem, rsem, lsem,
):
    row = lax.axis_index("rows")
    col = lax.axis_index("cols")
    y = row // nz
    z = lax.rem(row, nz)
    half = acc_a.shape[-1]

    load = pltpu.make_async_copy(items.at[row], mine, lsem)
    load.start()

    def along_z(d):
        other = lax.rem(z + d, nz)
        return other, {"rows": y * nz + other}

    def along_y(d):
        other = lax.rem(y + d, ny)
        return other, {"rows": other * nz + z}

    def along_c(d):
        other = lax.rem(col + d, nc)
        return other, {"cols": other}

    barrier = pltpu.get_barrier_semaphore()
    for size, along in ((nz, along_z), (ny, along_y), (nc, along_c)):
        for d in range(1, size):
            pl.semaphore_signal(barrier, inc=1, device_id=along(d)[1], device_id_type=MESH)
    pl.semaphore_wait(barrier, nz + ny + nc - 3)

    def push(src, dst, which, device):
        copy = pltpu.make_async_remote_copy(
            src_ref=src, dst_ref=dst, send_sem=ssem.at[which], recv_sem=rsem.at[which],
            device_id=device, device_id_type=MESH,
        )
        copy.start()

    def whole(src, dst, which):
        return pltpu.make_async_remote_copy(
            src_ref=src, dst_ref=dst, send_sem=ssem.at[which], recv_sem=rsem.at[which],
            device_id={"cols": lax.rem(col + 1, nc)}, device_id_type=MESH,
        )

    for d in range(1, max(ny, nz)):
        if d < nz:
            other, device = along_z(d)
            send_a[d - 1] = grad[:, other, :, :half].astype(BF16)
            push(send_a.at[d - 1], recv_a.at[d - 1], 0, device)
        if d < ny:
            other, device = along_y(d)
            send_b[d - 1] = grad[other, :, :, half:]
            push(send_b.at[d - 1], recv_b.at[d - 1], 1, device)

    whole(send_b, recv_b, 1).wait_recv()
    total = grad[y, :, :, half:]
    for d in range(ny - 1):
        total = total + recv_b[d]
    acc_b[...] = total
    for d in range(1, nz):
        other, device = along_z(d)
        push(acc_b.at[other], recv2_b.at[d - 1], 2, device)

    whole(send_a, recv_a, 0).wait_recv()
    total = grad[:, z, :, :half]
    for d in range(nz - 1):
        total = total + recv_a[d].astype(F32)
    acc_a[...] = total
    for d in range(1, ny):
        other, device = along_y(d)
        push(acc_a.at[other], recv2_a.at[d - 1], 3, device)

    whole(acc_b.at[pl.ds(0, nz - 1)], recv2_b, 2).wait_recv()
    own_b = acc_b[z]
    for d in range(nz - 1):
        own_b = own_b + recv2_b[d]
    whole(acc_a.at[pl.ds(0, ny - 1)], recv2_a, 3).wait_recv()
    own_a = acc_a[y]
    for d in range(ny - 1):
        own_a = own_a + recv2_a[d]

    part = jnp.sum(own_a * own_a + own_b * own_b, axis=0, keepdims=True)
    for n, (size, along, recv) in enumerate(
        ((nz, along_z, recv_z), (ny, along_y, recv_y), (nc, along_c, recv_c))
    ):
        sq[n] = part
        for d in range(1, size):
            push(sq.at[n], recv.at[d - 1], 4 + n, along(d)[1])
        whole(recv, recv, 4 + n).wait_recv()
        for d in range(size - 1):
            part = part + recv[d]
    entries = nc * ny * nz * out.shape[0] * out.shape[1]
    meansq = jnp.sum(part, axis=1, keepdims=True) / entries
    root = jnp.sqrt(meansq + 1e-06)

    load.wait()
    mixed = mine[...].astype(F32)
    out[:, :half] = mixed[:, :half] - 0.5 * own_a / root
    out[:, half:] = mixed[:, half:] - 0.5 * own_b / root

    whole(send_a, recv_a, 0).wait_send()
    whole(send_b, recv_b, 1).wait_send()
    whole(acc_b.at[pl.ds(0, nz - 1)], recv2_b, 2).wait_send()
    whole(acc_a.at[pl.ds(0, ny - 1)], recv2_a, 3).wait_send()
    for n, recv in enumerate((recv_z, recv_y, recv_c)):
        whole(recv, recv, 4 + n).wait_send()


def shards(
    users, items, ratings, tile_users, tile_items, tile_count, send_list, block_target, similarity
):
    icount, rank = items.shape[1:]
    tile = ratings.shape[-1]
    slots = ratings.shape[2]
    blocks = similarity.shape[2]
    ntiles = icount // tile
    nrows = lax.axis_size("rows")
    ncols = lax.axis_size("cols")
    nz = NZ
    ny = nrows // nz
    chunk = icount // nrows
    half = rank // 2
    panels = items[0].reshape(ntiles, tile, rank)
    smem = pl.BlockSpec(memory_space=pltpu.SMEM)
    vmem = pl.BlockSpec(memory_space=VMEM)
    grad_shape = jax.ShapeDtypeStruct((ntiles, tile, rank), F32)

    outgoing = panels[send_list[0, 0].reshape(-1)]
    incoming = lax.all_to_all(outgoing, "cols", split_axis=0, concat_axis=0, tiled=True)

    grad = pl.pallas_call(
        tiles_kernel,
        out_shape=grad_shape,
        in_specs=[smem, smem, smem, vmem, vmem, vmem],
        out_specs=vmem,
        compiler_params=pltpu.CompilerParams(vmem_limit_bytes=32 << 20),
        cost_estimate=pl.CostEstimate(
            flops=4 * slots * tile * tile * rank,
            bytes_accessed=2 * (users.size + items.size + ratings.size) + 4 * icount * rank,
            transcendentals=0,
        ),
        name="rating_tiles",
    )(
        tile_users[0, 0], tile_items[0, 0], tile_count[0],
        users.reshape(-1, tile, rank), panels, ratings[0, 0],
    )
    grad = pl.pallas_call(
        functools.partial(graph_kernel, blocks),
        out_shape=grad_shape,
        in_specs=[smem, vmem, vmem, vmem],
        out_specs=vmem,
        compiler_params=pltpu.CompilerParams(vmem_limit_bytes=32 << 20),
        name="graph_blocks",
    )(block_target[0, 0], similarity[0, 0], incoming.reshape(blocks, tile, rank), grad)

    updated = pl.pallas_call(
        functools.partial(reduce_kernel, ny, nz, ncols),
        out_shape=jax.ShapeDtypeStruct((chunk, rank), F32),
        in_specs=[vmem, pl.BlockSpec(memory_space=pl.ANY)],
        out_specs=vmem,
        scratch_shapes=[
            VMEM((nz - 1, ny, chunk, half), BF16),
            VMEM((ny - 1, nz, chunk, half), F32),
            VMEM((nz - 1, ny, chunk, half), BF16),
            VMEM((ny - 1, nz, chunk, half), F32),
            VMEM((ny, chunk, half), F32),
            VMEM((nz, chunk, half), F32),
            VMEM((ny - 1, chunk, half), F32),
            VMEM((nz - 1, chunk, half), F32),
            VMEM((3, 1, half), F32),
            VMEM((nz - 1, 1, half), F32),
            VMEM((ny - 1, 1, half), F32),
            VMEM((ncols - 1, 1, half), F32),
            VMEM((chunk, rank), BF16),
            pltpu.SemaphoreType.DMA((7,)),
            pltpu.SemaphoreType.DMA((7,)),
            pltpu.SemaphoreType.DMA,
        ],
        compiler_params=pltpu.CompilerParams(
            collective_id=0, has_side_effects=True, vmem_limit_bytes=32 << 20
        ),
        name="reduce_update",
    )(grad.reshape(ny, nz, chunk, rank), items[0].reshape(nrows, chunk, rank))
    return updated[None]


def solution(mesh):
    in_specs = (
        P("rows", None),
        P("cols", None, None),
        P("rows", "cols", None, None, None),
        P("rows", "cols", None),
        P("rows", "cols", None),
        P("rows", "cols"),
        P("rows", "cols", None, None),
        P("rows", "cols", None),
        P("rows", "cols", None, None, None),
    )
    out_specs = P("cols", "rows", None)
    return jax.shard_map(shards, mesh=mesh, in_specs=in_specs, out_specs=out_specs, check_vma=False)
```

```python
import functools

import jax
import jax.numpy as jnp
from jax import lax
from jax.experimental import pallas as pl
from jax.experimental.pallas import tpu as pltpu
from jax.sharding import PartitionSpec as P

NZ = 12
CORES = 2
UNROLL = 8
MESH = pl.DeviceIdType.MESH
VMEM = pltpu.VMEM
F32 = jnp.float32
BF16 = jnp.bfloat16


def kernel(
    ny, nz, nx,
    tu, ti, cnt, sl, tg, users_hbm, items_hbm, ratings_hbm, sim_hbm, chunks_hbm,
    out,
    users, items, ratings, sim, mine, users_t, picked, incoming, parts, grad,
    send_a, send_b, recv_a, recv_b, acc_a, acc_b, recv2_a, recv2_b,
    squares, recv_p, recv_q,
    ssem, rsem, lsem,
):
    row = lax.axis_index("rows")
    col = lax.axis_index("cols")
    y = row // nz
    z = lax.rem(row, nz)
    x = col // CORES
    core = lax.rem(col, CORES)
    nc = nx * CORES
    slots, tile = ratings.shape[0], ratings.shape[1]
    rank = users.shape[-1]
    chunk = grad.shape[2]
    half = rank // 2
    ntiles = items.shape[0]
    zero = slots + nc

    def fetch(src, dst, which):
        copy = pltpu.make_async_copy(src, dst, lsem.at[which])
        copy.start()
        return copy

    group = slots // 4
    item_copy = fetch(items_hbm, items, 0)
    user_copy = fetch(users_hbm, users, 1)
    rating_copies = [
        fetch(ratings_hbm.at[pl.ds(g * group, group)], ratings.at[pl.ds(g * group, group)], 4 + g)
        for g in range(4)
    ]
    sim_copy = fetch(sim_hbm, sim, 2)
    mine_copy = fetch(chunks_hbm.at[row], mine, 3)

    def at(dy, dz, dx, dk):
        return {
            "rows": lax.rem(y + dy, ny) * nz + lax.rem(z + dz, nz),
            "cols": lax.rem(x + dx, nx) * CORES + lax.rem(core + dk, CORES),
        }

    along_z = [(lax.rem(z + d, nz), {"rows": y * nz + lax.rem(z + d, nz)}) for d in range(nz)]
    along_y = [(lax.rem(y + d, ny), {"rows": lax.rem(y + d, ny) * nz + z}) for d in range(ny)]
    along_c = [(lax.rem(col + d, nc), {"cols": lax.rem(col + d, nc)}) for d in range(nc)]
    first_ring = [at(0, n // CORES, 0, n % CORES) for n in range(1, nz * CORES)]
    second_ring = [at(n // nx, 0, n % nx, 0) for n in range(1, ny * nx)]

    barrier = pltpu.get_barrier_semaphore()
    partners = [o[1] for o in along_c[1:] + along_y[1:] + along_z[1:]]
    partners += [at(0, n // CORES, 0, n % CORES) for n in range(1, nz * CORES) if n % CORES and n // CORES]
    partners += [at(n // nx, 0, n % nx, 0) for n in range(1, ny * nx) if n % nx and n // nx]
    for device in partners:
        pl.semaphore_signal(barrier, inc=1, device_id=device, device_id_type=MESH)

    def push(src, dst, which, device):
        pltpu.make_async_remote_copy(
            src_ref=src, dst_ref=dst, send_sem=ssem.at[which], recv_sem=rsem.at[which],
            device_id=device, device_id_type=MESH,
        ).start()

    def whole(src, dst, which):
        return pltpu.make_async_remote_copy(
            src_ref=src, dst_ref=dst, send_sem=ssem.at[which], recv_sem=rsem.at[which],
            device_id=along_c[1][1], device_id_type=MESH,
        )

    item_copy.wait()
    for d in range(1, nc):
        picked[d - 1] = items[sl[along_c[d][0]]]
    pl.semaphore_wait(barrier, len(partners))
    for d in range(1, nc):
        push(picked.at[d - 1], incoming.at[d - 1], 0, along_c[d][1])

    parts[zero] = jnp.zeros((tile, rank), F32)
    user_copy.wait()
    for i in range(users.shape[0]):
        users_t[i] = users[i].T
    count = cnt[0]

    def link(last, item, place):
        before = jnp.int32(zero)
        for i in range(ntiles):
            hit = item == i
            before = jnp.where(hit, last[i], before)
            last[i] = jnp.where(hit, place, last[i])
        return before

    def tiles(g, carry):
        last = list(carry)
        found = []
        for u in range(UNROLL):
            t = g * UNROLL + u
            user, item = tu[t], ti[t]
            pred = jnp.dot(items[item], users_t[user], preferred_element_type=F32)
            diff = pred - ratings[t].T.astype(F32)
            err = jnp.where(t < count, diff, 0.0).astype(BF16)
            found.append((t, item, jnp.dot(err, users[user], preferred_element_type=F32)))
        for t, item, part in found:
            parts[t] = part + parts[link(last, item, t)]
        return tuple(last)

    last = tuple(jnp.int32(zero) for _ in range(ntiles))
    steps = group // UNROLL
    for g in range(4):
        rating_copies[g].wait()
        last = lax.fori_loop(g * steps, (g + 1) * steps, tiles, last)

    last = list(last)
    sim_copy.wait()
    for d in range(nc):
        source = lax.rem(col + nc - d, nc)
        if d == 0:
            panel = items[sl[source]]
        else:
            if d == 1:
                whole(picked, incoming, 0).wait_recv()
            panel = incoming[d - 1]
        part = jnp.dot(sim[source], panel, preferred_element_type=F32)
        parts[slots + d] = part + parts[link(last, tg[source], slots + d)]
    per_tile = tile // chunk
    for i in range(ntiles):
        value = parts[last[i]]
        for j in range(per_tile):
            n = i * per_tile + j
            grad[n // nz, n % nz] = value[j * chunk:(j + 1) * chunk]

    for d in range(1, max(ny, nz)):
        if d < nz:
            other, device = along_z[d]
            send_a[d - 1] = grad[:, other, :, :half].astype(BF16)
            push(send_a.at[d - 1], recv_a.at[d - 1], 1, device)
        if d < ny:
            other, device = along_y[d]
            send_b[d - 1] = grad[other, :, :, half:]
            push(send_b.at[d - 1], recv_b.at[d - 1], 2, device)

    whole(send_b, recv_b, 2).wait_recv()
    total = grad[y, :, :, half:]
    for d in range(ny - 1):
        total = total + recv_b[d]
    acc_b[...] = total
    for d in range(1, nz):
        push(acc_b.at[along_z[d][0]], recv2_b.at[d - 1], 3, along_z[d][1])

    whole(send_a, recv_a, 1).wait_recv()
    total = grad[:, z, :, :half]
    for d in range(nz - 1):
        total = total + recv_a[d].astype(F32)
    acc_a[...] = total
    for d in range(1, ny):
        push(acc_a.at[along_y[d][0]], recv2_a.at[d - 1], 4, along_y[d][1])

    whole(acc_b.at[pl.ds(0, nz - 1)], recv2_b, 3).wait_recv()
    own_b = acc_b[z]
    for d in range(nz - 1):
        own_b = own_b + recv2_b[d]
    whole(acc_a.at[pl.ds(0, ny - 1)], recv2_a, 4).wait_recv()
    own_a = acc_a[y]
    for d in range(ny - 1):
        own_a = own_a + recv2_a[d]

    part = jnp.sum(own_a * own_a + own_b * own_b, axis=0, keepdims=True)
    for n, (ring, recv) in enumerate(((first_ring, recv_p), (second_ring, recv_q))):
        squares[n] = part
        for d, device in enumerate(ring):
            push(squares.at[n], recv.at[d], 5 + n, device)
        whole(recv, recv, 5 + n).wait_recv()
        part = part + jnp.sum(recv[...], axis=0)
    entries = nc * ny * nz * chunk * rank
    root = jnp.sqrt(jnp.sum(part, axis=1, keepdims=True) / entries + 1e-06)

    mine_copy.wait()
    mixed = mine[...].astype(F32)
    out[:, :half] = mixed[:, :half] - 0.5 * own_a / root
    out[:, half:] = mixed[:, half:] - 0.5 * own_b / root

    whole(picked, incoming, 0).wait_send()
    whole(send_a, recv_a, 1).wait_send()
    whole(send_b, recv_b, 2).wait_send()
    whole(acc_b.at[pl.ds(0, nz - 1)], recv2_b, 3).wait_send()
    whole(acc_a.at[pl.ds(0, ny - 1)], recv2_a, 4).wait_send()
    whole(recv_p, recv_p, 5).wait_send()
    whole(recv_q, recv_q, 6).wait_send()


def shards(
    users, items, ratings, tile_users, tile_items, tile_count, send_list, block_target, similarity
):
    icount, rank = items.shape[1:]
    tile = ratings.shape[-1]
    slots = ratings.shape[2]
    ntiles = icount // tile
    utiles = users.shape[0] // tile
    nrows = lax.axis_size("rows")
    nc = lax.axis_size("cols")
    nz, ny, nx = NZ, nrows // NZ, nc // CORES
    chunk = icount // nrows
    half = rank // 2
    smem = pl.BlockSpec(memory_space=pltpu.SMEM)
    hbm = pl.BlockSpec(memory_space=pltpu.HBM)

    updated = pl.pallas_call(
        functools.partial(kernel, ny, nz, nx),
        out_shape=jax.ShapeDtypeStruct((chunk, rank), F32),
        in_specs=[smem] * 5 + [hbm] * 5,
        out_specs=pl.BlockSpec(memory_space=VMEM),
        scratch_shapes=[
            VMEM((utiles, tile, rank), BF16),
            VMEM((ntiles, tile, rank), BF16),
            VMEM((slots, tile, tile), BF16),
            VMEM((nc, tile, tile), BF16),
            VMEM((chunk, rank), BF16),
            VMEM((utiles, rank, tile), BF16),
            VMEM((nc - 1, tile, rank), BF16),
            VMEM((nc - 1, tile, rank), BF16),
            VMEM((slots + nc + 1, tile, rank), F32),
            VMEM((ny, nz, chunk, rank), F32),
            VMEM((nz - 1, ny, chunk, half), BF16),
            VMEM((ny - 1, nz, chunk, half), F32),
            VMEM((nz - 1, ny, chunk, half), BF16),
            VMEM((ny - 1, nz, chunk, half), F32),
            VMEM((ny, chunk, half), F32),
            VMEM((nz, chunk, half), F32),
            VMEM((ny - 1, chunk, half), F32),
            VMEM((nz - 1, chunk, half), F32),
            VMEM((2, 1, half), F32),
            VMEM((nz * CORES - 1, 1, half), F32),
            VMEM((ny * nx - 1, 1, half), F32),
            pltpu.SemaphoreType.DMA((7,)),
            pltpu.SemaphoreType.DMA((7,)),
            pltpu.SemaphoreType.DMA((8,)),
        ],
        compiler_params=pltpu.CompilerParams(
            collective_id=0, has_side_effects=True, vmem_limit_bytes=60 << 20
        ),
        name="item_update",
    )(
        tile_users[0, 0], tile_items[0, 0], tile_count[0],
        send_list[0, 0].reshape(-1), block_target[0, 0],
        users.reshape(-1, tile, rank), items[0].reshape(-1, tile, rank),
        ratings[0, 0], similarity[0, 0], items[0].reshape(nrows, chunk, rank),
    )
    return updated[None]


def solution(mesh):
    in_specs = (
        P("rows", None),
        P("cols", None, None),
        P("rows", "cols", None, None, None),
        P("rows", "cols", None),
        P("rows", "cols", None),
        P("rows", "cols"),
        P("rows", "cols", None, None),
        P("rows", "cols", None),
        P("rows", "cols", None, None, None),
    )
    out_specs = P("cols", "rows", None)
    return jax.shard_map(shards, mesh=mesh, in_specs=in_specs, out_specs=out_specs, check_vma=False)
```

```python
import functools

import jax
import jax.numpy as jnp
from jax import lax
from jax.experimental import pallas as pl
from jax.experimental.pallas import tpu as pltpu
from jax.sharding import PartitionSpec as P

NZ = 12
CORES = 2
UNROLL = 8
MESH = pl.DeviceIdType.MESH
VMEM = pltpu.VMEM
F32 = jnp.float32
BF16 = jnp.bfloat16
I16 = jnp.int16
LEVELS = 32000.0


def kernel(
    ny, nz, nx,
    tu, ti, cnt, sl, tg, users_hbm, items_hbm, ratings_hbm, sim_hbm, chunks_hbm,
    out,
    users, items, ratings, sim, mine, users_t, picked, incoming, parts, grad_a, grad_b,
    send_a, send_b, recv_a, recv_b, acc_a, acc_b, send2_b, recv2_a, recv2_b,
    squares, recv_p, recv_q, steps, step_a, step_b, step2_b,
    ssem, rsem, lsem,
):
    row = lax.axis_index("rows")
    col = lax.axis_index("cols")
    y = row // nz
    z = lax.rem(row, nz)
    x = col // CORES
    core = lax.rem(col, CORES)
    nc = nx * CORES
    slots, tile = ratings.shape[0], ratings.shape[1]
    rank = users.shape[-1]
    chunk = grad_a.shape[2]
    half = rank // 2
    ntiles = items.shape[0]
    zero = slots + nc

    def fetch(src, dst, which):
        copy = pltpu.make_async_copy(src, dst, lsem.at[which])
        copy.start()
        return copy

    group = slots // 4
    item_copy = fetch(items_hbm, items, 0)
    user_copy = fetch(users_hbm, users, 1)
    rating_copies = [
        fetch(ratings_hbm.at[pl.ds(g * group, group)], ratings.at[pl.ds(g * group, group)], 4 + g)
        for g in range(4)
    ]
    sim_copy = fetch(sim_hbm, sim, 2)
    mine_copy = fetch(chunks_hbm.at[row], mine, 3)

    def at(dy, dz, dx, dk):
        return {
            "rows": lax.rem(y + dy, ny) * nz + lax.rem(z + dz, nz),
            "cols": lax.rem(x + dx, nx) * CORES + lax.rem(core + dk, CORES),
        }

    along_z = [(lax.rem(z + d, nz), {"rows": y * nz + lax.rem(z + d, nz)}) for d in range(nz)]
    along_y = [(lax.rem(y + d, ny), {"rows": lax.rem(y + d, ny) * nz + z}) for d in range(ny)]
    along_c = [(lax.rem(col + d, nc), {"cols": lax.rem(col + d, nc)}) for d in range(nc)]

    def hops(d, size):
        return min(d, size - d)

    z_order = sorted(range(1, nz), key=lambda d: -hops(d, nz))
    y_order = sorted(range(1, ny), key=lambda d: -hops(d, ny))
    first = [(d, k) for d in range(nz) for k in range(CORES)][1:]
    first.sort(key=lambda p: -hops(p[0], nz) - 0.3 * p[1])
    second = [(d, e) for d in range(ny) for e in range(nx)][1:]
    second.sort(key=lambda p: -hops(p[0], ny) - hops(p[1], nx))
    first_ring = [at(0, d, 0, k) for d, k in first]
    second_ring = [at(d, 0, e, 0) for d, e in second]

    barrier = pltpu.get_barrier_semaphore()
    partners = [o[1] for o in along_c[1:] + along_y[1:] + along_z[1:]]
    for device in partners:
        pl.semaphore_signal(barrier, inc=1, device_id=device, device_id_type=MESH)

    def push(src, dst, which, device):
        pltpu.make_async_remote_copy(
            src_ref=src, dst_ref=dst, send_sem=ssem.at[which], recv_sem=rsem.at[which],
            device_id=device, device_id_type=MESH,
        ).start()

    def whole(src, dst, which):
        return pltpu.make_async_remote_copy(
            src_ref=src, dst_ref=dst, send_sem=ssem.at[which], recv_sem=rsem.at[which],
            device_id=along_c[1][1], device_id_type=MESH,
        )

    item_copy.wait()
    for d in range(1, nc):
        panel = items[sl[along_c[d][0]]]
        picked[0, d - 1] = panel[:, :half]
        picked[1, d - 1] = panel[:, half:]
    pl.semaphore_wait(barrier, len(partners))

    def send_panels(h):
        for d in range(1, nc):
            push(picked.at[h, d - 1], incoming.at[h, d - 1], h, along_c[d][1])

    send_panels(0)

    parts[zero] = jnp.zeros((tile, rank), F32)
    user_copy.wait()
    for i in range(users.shape[0]):
        users_t[i] = users[i].T
    count = cnt[0]

    def link(last, item, place):
        before = jnp.int32(zero)
        for i in range(ntiles):
            hit = item == i
            before = jnp.where(hit, last[i], before)
            last[i] = jnp.where(hit, place, last[i])
        return before

    def tiles(g, carry):
        last = list(carry)
        found = []
        for u in range(UNROLL):
            t = g * UNROLL + u
            user, item = tu[t], ti[t]
            pred = jnp.dot(items[item], users_t[user], preferred_element_type=F32)
            diff = pred - ratings[t].T.astype(F32)
            err = jnp.where(t < count, diff, 0.0).astype(BF16)
            found.append((t, item, jnp.dot(err, users[user], preferred_element_type=F32)))
        for t, item, part in found:
            parts[t] = part + parts[link(last, item, t)]
        return tuple(last)

    last = tuple(jnp.int32(zero) for _ in range(ntiles))
    turns = group // UNROLL
    for g in range(4):
        rating_copies[g].wait()
        if g == 2:
            whole(picked.at[0], incoming.at[0], 0).wait_send()
            send_panels(1)
        last = lax.fori_loop(g * turns, (g + 1) * turns, tiles, last)

    last = list(last)
    sources = [lax.rem(col + nc - d, nc) for d in range(nc)]
    before = [link(last, tg[sources[d]], slots + d) for d in range(nc)]
    sim_copy.wait()
    parts[slots] = parts[before[0]] + jnp.dot(
        sim[sources[0]], items[sl[col]], preferred_element_type=F32
    )

    def finish(h, grad):
        cut = slice(h * half, (h + 1) * half)
        whole(picked.at[h], incoming.at[h], h).wait_recv()
        for d in range(1, nc):
            part = jnp.dot(sim[sources[d]], incoming[h, d - 1], preferred_element_type=F32)
            parts[slots + d, :, cut] = part + parts[before[d], :, cut]
        top = jnp.zeros((8, half), F32)
        for i in range(ntiles):
            value = parts[last[i], :, cut]
            top = jnp.maximum(top, jnp.max(jnp.abs(value).reshape(tile // 8, 8, half), axis=0))
            for j in range(tile // chunk):
                n = i * (tile // chunk) + j
                grad[n // nz, n % nz] = value[j * chunk:(j + 1) * chunk]
        return step_of(top)

    def step_of(top):
        top = jnp.max(jnp.max(top, axis=0, keepdims=True), axis=1, keepdims=True)
        return jnp.maximum(top, 1e-20) / LEVELS

    def code(value, inverse):
        return jnp.round(value * inverse).astype(jnp.int32).astype(I16)

    step = finish(0, grad_a)
    steps[0] = jnp.broadcast_to(step, (1, half))
    inverse = 1.0 / step
    for d in z_order:
        other, device = along_z[d]
        push(steps.at[0], step_a.at[d - 1], 7, device)
        send_a[d - 1] = code(grad_a[:, other], inverse)
        push(send_a.at[d - 1], recv_a.at[d - 1], 2, device)
    step = finish(1, grad_b)
    steps[1] = jnp.broadcast_to(step, (1, half))
    inverse = 1.0 / step
    for d in y_order:
        other, device = along_y[d]
        push(steps.at[1], step_b.at[d - 1], 8, device)
        send_b[d - 1] = code(grad_b[other], inverse)
        push(send_b.at[d - 1], recv_b.at[d - 1], 3, device)

    whole(step_b, step_b, 8).wait_recv()
    whole(send_b, recv_b, 3).wait_recv()
    total = grad_b[y]
    for d in range(ny - 1):
        total = total + recv_b[d].astype(F32) * step_b[d]
    acc_b[...] = total
    step = step_of(jnp.max(jnp.abs(total).reshape(-1, 8, half), axis=0))
    steps[2] = jnp.broadcast_to(step, (1, half))
    send2_b[...] = code(total, 1.0 / step)
    for d in z_order:
        push(steps.at[2], step2_b.at[d - 1], 9, along_z[d][1])
        push(send2_b.at[along_z[d][0]], recv2_b.at[d - 1], 4, along_z[d][1])

    whole(step_a, step_a, 7).wait_recv()
    whole(send_a, recv_a, 2).wait_recv()
    total = grad_a[:, z]
    for d in range(nz - 1):
        total = total + recv_a[d].astype(F32) * step_a[d]
    acc_a[...] = total
    for d in y_order:
        push(acc_a.at[along_y[d][0]], recv2_a.at[d - 1], 10, along_y[d][1])

    whole(step2_b, step2_b, 9).wait_recv()
    whole(send2_b.at[pl.ds(0, nz - 1)], recv2_b, 4).wait_recv()
    own_b = acc_b[z]
    for d in range(nz - 1):
        own_b = own_b + recv2_b[d].astype(F32) * step2_b[d]
    whole(acc_a.at[pl.ds(0, ny - 1)], recv2_a, 10).wait_recv()
    own_a = acc_a[y]
    for d in range(ny - 1):
        own_a = own_a + recv2_a[d]

    part = jnp.sum(own_a * own_a + own_b * own_b, axis=0, keepdims=True)
    for n, (ring, recv) in enumerate(((first_ring, recv_p), (second_ring, recv_q))):
        squares[n] = part
        for d, device in enumerate(ring):
            push(squares.at[n], recv.at[d], 5 + n, device)
        whole(recv, recv, 5 + n).wait_recv()
        part = part + jnp.sum(recv[...], axis=0)
    entries = nc * ny * nz * chunk * rank
    root = jnp.sqrt(jnp.sum(part, axis=1, keepdims=True) / entries + 1e-06)

    mine_copy.wait()
    mixed = mine[...].astype(F32)
    out[:, :half] = mixed[:, :half] - 0.5 * own_a / root
    out[:, half:] = mixed[:, half:] - 0.5 * own_b / root

    whole(picked.at[1], incoming.at[1], 1).wait_send()
    whole(send_a, recv_a, 2).wait_send()
    whole(send_b, recv_b, 3).wait_send()
    whole(send2_b.at[pl.ds(0, nz - 1)], recv2_b, 4).wait_send()
    whole(acc_a.at[pl.ds(0, ny - 1)], recv2_a, 10).wait_send()
    whole(recv_p, recv_p, 5).wait_send()
    whole(recv_q, recv_q, 6).wait_send()
    whole(step_a, step_a, 7).wait_send()
    whole(step_b, step_b, 8).wait_send()
    whole(step2_b, step2_b, 9).wait_send()


def shards(
    users, items, ratings, tile_users, tile_items, tile_count, send_list, block_target, similarity
):
    icount, rank = items.shape[1:]
    tile = ratings.shape[-1]
    slots = ratings.shape[2]
    ntiles = icount // tile
    utiles = users.shape[0] // tile
    nrows = lax.axis_size("rows")
    nc = lax.axis_size("cols")
    nz, ny, nx = NZ, nrows // NZ, nc // CORES
    chunk = icount // nrows
    half = rank // 2
    smem = pl.BlockSpec(memory_space=pltpu.SMEM)
    hbm = pl.BlockSpec(memory_space=pltpu.HBM)

    updated = pl.pallas_call(
        functools.partial(kernel, ny, nz, nx),
        out_shape=jax.ShapeDtypeStruct((chunk, rank), F32),
        in_specs=[smem] * 5 + [hbm] * 5,
        out_specs=pl.BlockSpec(memory_space=VMEM),
        scratch_shapes=[
            VMEM((utiles, tile, rank), BF16),
            VMEM((ntiles, tile, rank), BF16),
            VMEM((slots, tile, tile), BF16),
            VMEM((nc, tile, tile), BF16),
            VMEM((chunk, rank), BF16),
            VMEM((utiles, rank, tile), BF16),
            VMEM((2, nc - 1, tile, half), BF16),
            VMEM((2, nc - 1, tile, half), BF16),
            VMEM((slots + nc + 1, tile, rank), F32),
            VMEM((ny, nz, chunk, half), F32),
            VMEM((ny, nz, chunk, half), F32),
            VMEM((nz - 1, ny, chunk, half), I16),
            VMEM((ny - 1, nz, chunk, half), I16),
            VMEM((nz - 1, ny, chunk, half), I16),
            VMEM((ny - 1, nz, chunk, half), I16),
            VMEM((ny, chunk, half), F32),
            VMEM((nz, chunk, half), F32),
            VMEM((nz, chunk, half), I16),
            VMEM((ny - 1, chunk, half), F32),
            VMEM((nz - 1, chunk, half), I16),
            VMEM((2, 1, half), F32),
            VMEM((nz * CORES - 1, 1, half), F32),
            VMEM((ny * nx - 1, 1, half), F32),
            VMEM((3, 1, half), F32),
            VMEM((nz - 1, 1, half), F32),
            VMEM((ny - 1, 1, half), F32),
            VMEM((nz - 1, 1, half), F32),
            pltpu.SemaphoreType.DMA((11,)),
            pltpu.SemaphoreType.DMA((11,)),
            pltpu.SemaphoreType.DMA((8,)),
        ],
        compiler_params=pltpu.CompilerParams(
            collective_id=0, has_side_effects=True, vmem_limit_bytes=60 << 20
        ),
        name="item_update",
    )(
        tile_users[0, 0], tile_items[0, 0], tile_count[0],
        send_list[0, 0].reshape(-1), block_target[0, 0],
        users.reshape(-1, tile, rank), items[0].reshape(-1, tile, rank),
        ratings[0, 0], similarity[0, 0], items[0].reshape(nrows, chunk, rank),
    )
    return updated[None]


def solution(mesh):
    in_specs = (
        P("rows", None),
        P("cols", None, None),
        P("rows", "cols", None, None, None),
        P("rows", "cols", None),
        P("rows", "cols", None),
        P("rows", "cols"),
        P("rows", "cols", None, None),
        P("rows", "cols", None),
        P("rows", "cols", None, None, None),
    )
    out_specs = P("cols", "rows", None)
    return jax.shard_map(shards, mesh=mesh, in_specs=in_specs, out_specs=out_specs, check_vma=False)
```

```python
import functools

import jax
import jax.numpy as jnp
from jax import lax
from jax.experimental import pallas as pl
from jax.experimental.pallas import tpu as pltpu
from jax.sharding import PartitionSpec as P

NZ = 12
CORES = 2
UNROLL = 8
MESH = pl.DeviceIdType.MESH
VMEM = pltpu.VMEM
F32 = jnp.float32
BF16 = jnp.bfloat16
I16 = jnp.int16
LEVELS = 32000.0


def kernel(
    ny, nz, nx,
    cnt, tu_hbm, ti_hbm, sl_hbm, tg_hbm, users_hbm, items_hbm, ratings_hbm, sim_hbm, chunks_hbm,
    out,
    tu, ti, sl, tg, users, items, ratings, sim, mine, users_t, picked, incoming, parts, grad_a, grad_b,
    send_a, send_b, recv_a, recv_b, acc_a, acc_b, send2_b, recv2_a, recv2_b,
    squares, recv_p, recv_q, steps, step_a, step_b, step2_b,
    ssem, rsem, lsem,
):
    row = lax.axis_index("rows")
    col = lax.axis_index("cols")
    y = row // nz
    z = lax.rem(row, nz)
    x = col // CORES
    core = lax.rem(col, CORES)
    nc = nx * CORES
    slots, tile = ratings.shape[0], ratings.shape[1]
    rank = users.shape[-1]
    chunk = grad_a.shape[2]
    half = rank // 2
    ntiles = items.shape[0]
    zero = slots + nc

    def fetch(src, dst, which):
        copy = pltpu.make_async_copy(src, dst, lsem.at[which])
        copy.start()
        return copy

    group = slots // 4
    list_copy = fetch(sl_hbm, sl, 8)
    item_copy = fetch(items_hbm, items, 0)
    user_copy = fetch(users_hbm, users, 1)
    rating_copies = [
        fetch(ratings_hbm.at[pl.ds(g * group, group)], ratings.at[pl.ds(g * group, group)], 4 + g)
        for g in range(4)
    ]
    index_copies = [
        fetch(src, dst, 9 + n)
        for n, (src, dst) in enumerate(((tu_hbm, tu), (ti_hbm, ti), (tg_hbm, tg)))
    ]
    sim_copy = fetch(sim_hbm, sim, 2)
    mine_copy = fetch(chunks_hbm.at[row], mine, 3)

    def at(dy, dz, dx, dk):
        return {
            "rows": lax.rem(y + dy, ny) * nz + lax.rem(z + dz, nz),
            "cols": lax.rem(x + dx, nx) * CORES + lax.rem(core + dk, CORES),
        }

    along_z = [(lax.rem(z + d, nz), {"rows": y * nz + lax.rem(z + d, nz)}) for d in range(nz)]
    along_y = [(lax.rem(y + d, ny), {"rows": lax.rem(y + d, ny) * nz + z}) for d in range(ny)]
    along_c = [(lax.rem(col + d, nc), {"cols": lax.rem(col + d, nc)}) for d in range(nc)]

    def hops(d, size):
        return min(d, size - d)

    z_order = sorted(range(1, nz), key=lambda d: -hops(d, nz))
    y_order = sorted(range(1, ny), key=lambda d: -hops(d, ny))
    first = [(d, k) for d in range(nz) for k in range(CORES)][1:]
    first.sort(key=lambda p: -hops(p[0], nz) - 0.3 * p[1])
    second = [(d, e) for d in range(ny) for e in range(nx)][1:]
    second.sort(key=lambda p: -hops(p[0], ny) - hops(p[1], nx))
    first_ring = [at(0, d, 0, k) for d, k in first]
    second_ring = [at(d, 0, e, 0) for d, e in second]

    barrier = pltpu.get_barrier_semaphore()
    partners = [o[1] for o in along_c[1:] + along_y[1:] + along_z[1:]]
    for device in partners:
        pl.semaphore_signal(barrier, inc=1, device_id=device, device_id_type=MESH)

    def push(src, dst, which, device):
        pltpu.make_async_remote_copy(
            src_ref=src, dst_ref=dst, send_sem=ssem.at[which], recv_sem=rsem.at[which],
            device_id=device, device_id_type=MESH,
        ).start()

    def whole(src, dst, which):
        return pltpu.make_async_remote_copy(
            src_ref=src, dst_ref=dst, send_sem=ssem.at[which], recv_sem=rsem.at[which],
            device_id=along_c[1][1], device_id_type=MESH,
        )

    list_copy.wait()
    item_copy.wait()
    for d in range(1, nc):
        panel = items[sl[along_c[d][0]]]
        picked[0, d - 1] = panel[:, :half]
        picked[1, d - 1] = panel[:, half:]
    pl.semaphore_wait(barrier, len(partners))

    def send_panels(h):
        for d in range(1, nc):
            push(picked.at[h, d - 1], incoming.at[h, d - 1], h, along_c[d][1])

    send_panels(0)

    parts[zero] = jnp.zeros((tile, rank), F32)
    user_copy.wait()
    for i in range(users.shape[0]):
        users_t[i] = users[i].T
    for copy in index_copies:
        copy.wait()
    count = cnt[0]

    def link(last, item, place):
        before = jnp.int32(zero)
        for i in range(ntiles):
            hit = item == i
            before = jnp.where(hit, last[i], before)
            last[i] = jnp.where(hit, place, last[i])
        return before

    def tiles(g, carry):
        last = list(carry)
        found = []
        for u in range(UNROLL):
            t = g * UNROLL + u
            user, item = tu[t], ti[t]
            pred = jnp.dot(items[item], users_t[user], preferred_element_type=F32)
            diff = pred - ratings[t].T.astype(F32)
            err = jnp.where(t < count, diff, 0.0).astype(BF16)
            found.append((t, item, jnp.dot(err, users[user], preferred_element_type=F32)))
        for t, item, part in found:
            parts[t] = part + parts[link(last, item, t)]
        return tuple(last)

    last = tuple(jnp.int32(zero) for _ in range(ntiles))
    turns = group // UNROLL
    for g in range(4):
        rating_copies[g].wait()
        if g == 2:
            whole(picked.at[0], incoming.at[0], 0).wait_send()
            send_panels(1)
        last = lax.fori_loop(g * turns, (g + 1) * turns, tiles, last)

    last = list(last)
    sources = [lax.rem(col + nc - d, nc) for d in range(nc)]
    before = [link(last, tg[sources[d]], slots + d) for d in range(nc)]
    sim_copy.wait()
    parts[slots] = parts[before[0]] + jnp.dot(
        sim[sources[0]], items[sl[col]], preferred_element_type=F32
    )

    def finish(h, grad):
        cut = slice(h * half, (h + 1) * half)
        whole(picked.at[h], incoming.at[h], h).wait_recv()
        for d in range(1, nc):
            part = jnp.dot(sim[sources[d]], incoming[h, d - 1], preferred_element_type=F32)
            parts[slots + d, :, cut] = part + parts[before[d], :, cut]
        top = jnp.zeros((8, half), F32)
        for i in range(ntiles):
            value = parts[last[i], :, cut]
            top = jnp.maximum(top, jnp.max(jnp.abs(value).reshape(tile // 8, 8, half), axis=0))
            for j in range(tile // chunk):
                n = i * (tile // chunk) + j
                grad[n // nz, n % nz] = value[j * chunk:(j + 1) * chunk]
        return step_of(top)

    def step_of(top):
        top = jnp.max(jnp.max(top, axis=0, keepdims=True), axis=1, keepdims=True)
        return jnp.maximum(top, 1e-20) / LEVELS

    def code(value, inverse):
        return jnp.round(value * inverse).astype(jnp.int32).astype(I16)

    step = finish(0, grad_a)
    steps[0] = jnp.broadcast_to(step, (1, half))
    inverse = 1.0 / step
    for d in z_order:
        other, device = along_z[d]
        push(steps.at[0], step_a.at[d - 1], 7, device)
        send_a[d - 1] = code(grad_a[:, other], inverse)
        push(send_a.at[d - 1], recv_a.at[d - 1], 2, device)
    step = finish(1, grad_b)
    steps[1] = jnp.broadcast_to(step, (1, half))
    inverse = 1.0 / step
    for d in y_order:
        other, device = along_y[d]
        push(steps.at[1], step_b.at[d - 1], 8, device)
        send_b[d - 1] = code(grad_b[other], inverse)
        push(send_b.at[d - 1], recv_b.at[d - 1], 3, device)

    whole(step_b, step_b, 8).wait_recv()
    whole(send_b, recv_b, 3).wait_recv()
    total = grad_b[y]
    for d in range(ny - 1):
        total = total + recv_b[d].astype(F32) * step_b[d]
    acc_b[...] = total
    step = step_of(jnp.max(jnp.abs(total).reshape(-1, 8, half), axis=0))
    steps[2] = jnp.broadcast_to(step, (1, half))
    send2_b[...] = code(total, 1.0 / step)
    for d in z_order:
        push(steps.at[2], step2_b.at[d - 1], 9, along_z[d][1])
        push(send2_b.at[along_z[d][0]], recv2_b.at[d - 1], 4, along_z[d][1])

    whole(step_a, step_a, 7).wait_recv()
    whole(send_a, recv_a, 2).wait_recv()
    total = grad_a[:, z]
    for d in range(nz - 1):
        total = total + recv_a[d].astype(F32) * step_a[d]
    acc_a[...] = total
    for d in y_order:
        push(acc_a.at[along_y[d][0]], recv2_a.at[d - 1], 10, along_y[d][1])

    whole(step2_b, step2_b, 9).wait_recv()
    whole(send2_b.at[pl.ds(0, nz - 1)], recv2_b, 4).wait_recv()
    own_b = acc_b[z]
    for d in range(nz - 1):
        own_b = own_b + recv2_b[d].astype(F32) * step2_b[d]
    whole(acc_a.at[pl.ds(0, ny - 1)], recv2_a, 10).wait_recv()
    own_a = acc_a[y]
    for d in range(ny - 1):
        own_a = own_a + recv2_a[d]

    part = jnp.sum(own_a * own_a + own_b * own_b, axis=0, keepdims=True)
    for n, (ring, recv) in enumerate(((first_ring, recv_p), (second_ring, recv_q))):
        squares[n] = part
        for d, device in enumerate(ring):
            push(squares.at[n], recv.at[d], 5 + n, device)
        whole(recv, recv, 5 + n).wait_recv()
        part = part + jnp.sum(recv[...], axis=0)
    entries = nc * ny * nz * chunk * rank
    root = jnp.sqrt(jnp.sum(part, axis=1, keepdims=True) / entries + 1e-06)

    mine_copy.wait()
    mixed = mine[...].astype(F32)
    out[:, :half] = mixed[:, :half] - 0.5 * own_a / root
    out[:, half:] = mixed[:, half:] - 0.5 * own_b / root

    whole(picked.at[1], incoming.at[1], 1).wait_send()
    whole(send_a, recv_a, 2).wait_send()
    whole(send_b, recv_b, 3).wait_send()
    whole(send2_b.at[pl.ds(0, nz - 1)], recv2_b, 4).wait_send()
    whole(acc_a.at[pl.ds(0, ny - 1)], recv2_a, 10).wait_send()
    whole(recv_p, recv_p, 5).wait_send()
    whole(recv_q, recv_q, 6).wait_send()
    whole(step_a, step_a, 7).wait_send()
    whole(step_b, step_b, 8).wait_send()
    whole(step2_b, step2_b, 9).wait_send()


def shards(
    users, items, ratings, tile_users, tile_items, tile_count, send_list, block_target, similarity
):
    icount, rank = items.shape[1:]
    tile = ratings.shape[-1]
    slots = ratings.shape[2]
    ntiles = icount // tile
    utiles = users.shape[0] // tile
    nrows = lax.axis_size("rows")
    nc = lax.axis_size("cols")
    nz, ny, nx = NZ, nrows // NZ, nc // CORES
    chunk = icount // nrows
    half = rank // 2
    hbm = pl.BlockSpec(memory_space=pltpu.HBM)

    updated = pl.pallas_call(
        functools.partial(kernel, ny, nz, nx),
        out_shape=jax.ShapeDtypeStruct((chunk, rank), F32),
        in_specs=[pl.BlockSpec(memory_space=pltpu.SMEM)] + [hbm] * 9,
        out_specs=pl.BlockSpec(memory_space=VMEM),
        scratch_shapes=[
            pltpu.SMEM((slots,), jnp.int32),
            pltpu.SMEM((slots,), jnp.int32),
            pltpu.SMEM((nc,), jnp.int32),
            pltpu.SMEM((nc,), jnp.int32),
            VMEM((utiles, tile, rank), BF16),
            VMEM((ntiles, tile, rank), BF16),
            VMEM((slots, tile, tile), BF16),
            VMEM((nc, tile, tile), BF16),
            VMEM((chunk, rank), BF16),
            VMEM((utiles, rank, tile), BF16),
            VMEM((2, nc - 1, tile, half), BF16),
            VMEM((2, nc - 1, tile, half), BF16),
            VMEM((slots + nc + 1, tile, rank), F32),
            VMEM((ny, nz, chunk, half), F32),
            VMEM((ny, nz, chunk, half), F32),
            VMEM((nz - 1, ny, chunk, half), I16),
            VMEM((ny - 1, nz, chunk, half), I16),
            VMEM((nz - 1, ny, chunk, half), I16),
            VMEM((ny - 1, nz, chunk, half), I16),
            VMEM((ny, chunk, half), F32),
            VMEM((nz, chunk, half), F32),
            VMEM((nz, chunk, half), I16),
            VMEM((ny - 1, chunk, half), F32),
            VMEM((nz - 1, chunk, half), I16),
            VMEM((2, 1, half), F32),
            VMEM((nz * CORES - 1, 1, half), F32),
            VMEM((ny * nx - 1, 1, half), F32),
            VMEM((3, 1, half), F32),
            VMEM((nz - 1, 1, half), F32),
            VMEM((ny - 1, 1, half), F32),
            VMEM((nz - 1, 1, half), F32),
            pltpu.SemaphoreType.DMA((11,)),
            pltpu.SemaphoreType.DMA((11,)),
            pltpu.SemaphoreType.DMA((12,)),
        ],
        compiler_params=pltpu.CompilerParams(
            collective_id=0, has_side_effects=True, vmem_limit_bytes=40 << 20
        ),
        name="item_update",
    )(
        tile_count[0],
        *(
            pltpu.with_memory_space_constraint(a, pltpu.HBM)
            for a in (
                tile_users[0, 0], tile_items[0, 0], send_list[0, 0].reshape(-1), block_target[0, 0],
                users.reshape(-1, tile, rank), items[0].reshape(-1, tile, rank),
                ratings[0, 0], similarity[0, 0], items[0].reshape(nrows, chunk, rank),
            )
        ),
    )
    return updated[None]


def solution(mesh):
    in_specs = (
        P("rows", None),
        P("cols", None, None),
        P("rows", "cols", None, None, None),
        P("rows", "cols", None),
        P("rows", "cols", None),
        P("rows", "cols"),
        P("rows", "cols", None, None),
        P("rows", "cols", None),
        P("rows", "cols", None, None, None),
    )
    out_specs = P("cols", "rows", None)
    return jax.shard_map(shards, mesh=mesh, in_specs=in_specs, out_specs=out_specs, check_vma=False)
```

```python
import functools

import jax
import jax.numpy as jnp
from jax import lax
from jax.experimental import pallas as pl
from jax.experimental.pallas import tpu as pltpu
from jax.sharding import PartitionSpec as P

NZ = 12
CORES = 2
UNROLL = 16
MESH = pl.DeviceIdType.MESH
VMEM = pltpu.VMEM
F32 = jnp.float32
BF16 = jnp.bfloat16
I16 = jnp.int16
LEVELS = 32000.0


def kernel(
    ny, nz, nx,
    cnt, tu_hbm, ti_hbm, sl_hbm, tg_hbm, users_hbm, items_hbm, ratings_hbm, sim_hbm, chunks_hbm,
    out,
    tu, ti, sl, tg, users, items, ratings, sim, mine, users_t, picked, incoming, parts, grad_a, grad_b,
    send_a, send_b, recv_a, recv_b, acc_a, acc_b, send2_a, send2_b, recv2_a, recv2_b,
    squares, recv_p, recv_q, steps, step_a, step_b, step2_a, step2_b,
    ssem, rsem, lsem,
):
    row = lax.axis_index("rows")
    col = lax.axis_index("cols")
    y = row // nz
    z = lax.rem(row, nz)
    x = col // CORES
    core = lax.rem(col, CORES)
    nc = nx * CORES
    slots, tile = ratings.shape[0], ratings.shape[1]
    rank = users.shape[-1]
    chunk = grad_a.shape[2]
    half = rank // 2
    ntiles = items.shape[0]
    zero = slots + nc

    def fetch(src, dst, which):
        copy = pltpu.make_async_copy(src, dst, lsem.at[which])
        copy.start()
        return copy

    group = slots // 4
    list_copy = fetch(sl_hbm, sl, 8)
    item_copy = fetch(items_hbm, items, 0)

    def at(dy, dz, dx, dk):
        return {
            "rows": lax.rem(y + dy, ny) * nz + lax.rem(z + dz, nz),
            "cols": lax.rem(x + dx, nx) * CORES + lax.rem(core + dk, CORES),
        }

    along_z = [(lax.rem(z + d, nz), {"rows": y * nz + lax.rem(z + d, nz)}) for d in range(nz)]
    along_y = [(lax.rem(y + d, ny), {"rows": lax.rem(y + d, ny) * nz + z}) for d in range(ny)]
    along_c = [(lax.rem(col + d, nc), {"cols": lax.rem(col + d, nc)}) for d in range(nc)]

    def hops(d, size):
        return min(d, size - d)

    z_order = sorted(range(1, nz), key=lambda d: -hops(d, nz))
    c_order = sorted(range(1, nc), key=lambda d: -hops(d, nc))
    y_order = sorted(range(1, ny), key=lambda d: -hops(d, ny))
    first = [(d, k) for d in range(nz) for k in range(CORES)][1:]
    first.sort(key=lambda p: -hops(p[0], nz) - 0.3 * p[1])
    second = [(d, e) for d in range(ny) for e in range(nx)][1:]
    second.sort(key=lambda p: -hops(p[0], ny) - hops(p[1], nx))
    first_ring = [at(0, d, 0, k) for d, k in first]
    second_ring = [at(d, 0, e, 0) for d, e in second]

    barrier = pltpu.get_barrier_semaphore()
    partners = [o[1] for o in along_c[1:] + along_y[1:] + along_z[1:]]
    for device in partners:
        pl.semaphore_signal(barrier, inc=1, device_id=device, device_id_type=MESH)

    user_copy = fetch(users_hbm, users, 1)
    rating_copies = [
        fetch(ratings_hbm.at[pl.ds(g * group, group)], ratings.at[pl.ds(g * group, group)], 4 + g)
        for g in range(4)
    ]
    index_copies = [
        fetch(src, dst, 9 + n)
        for n, (src, dst) in enumerate(((tu_hbm, tu), (ti_hbm, ti), (tg_hbm, tg)))
    ]
    sim_copy = fetch(sim_hbm, sim, 2)
    mine_copy = fetch(chunks_hbm.at[row], mine, 3)

    def push(src, dst, which, device):
        pltpu.make_async_remote_copy(
            src_ref=src, dst_ref=dst, send_sem=ssem.at[which], recv_sem=rsem.at[which],
            device_id=device, device_id_type=MESH,
        ).start()

    def whole(src, dst, which):
        return pltpu.make_async_remote_copy(
            src_ref=src, dst_ref=dst, send_sem=ssem.at[which], recv_sem=rsem.at[which],
            device_id=along_c[1][1], device_id_type=MESH,
        )

    list_copy.wait()
    item_copy.wait()
    for d in range(1, nc):
        panel = items[sl[along_c[d][0]]]
        picked[0, d - 1] = panel[:, :half]
        picked[1, d - 1] = panel[:, half:]
    pl.semaphore_wait(barrier, len(partners))

    def send_panels(h):
        for d in c_order:
            push(picked.at[h, d - 1], incoming.at[h, d - 1], h, along_c[d][1])

    send_panels(0)

    parts[zero] = jnp.zeros((tile, rank), F32)
    user_copy.wait()
    for i in range(users.shape[0]):
        users_t[i] = users[i].T
    for copy in index_copies:
        copy.wait()
    count = cnt[0]

    def link(last, item, place):
        before = jnp.int32(zero)
        for i in range(ntiles):
            hit = item == i
            before = jnp.where(hit, last[i], before)
            last[i] = jnp.where(hit, place, last[i])
        return before

    def tiles(g, carry):
        last = list(carry)
        found = []
        for u in range(UNROLL):
            t = g * UNROLL + u
            user, item = tu[t], ti[t]
            pred = jnp.dot(items[item], users_t[user], preferred_element_type=F32)
            diff = pred - ratings[t].T.astype(F32)
            err = jnp.where(t < count, diff, 0.0).astype(BF16)
            found.append((t, item, jnp.dot(err, users[user], preferred_element_type=F32)))
        for t, item, part in found:
            parts[t] = part + parts[link(last, item, t)]
        return tuple(last)

    last = tuple(jnp.int32(zero) for _ in range(ntiles))
    turns = group // UNROLL
    for g in range(4):
        rating_copies[g].wait()
        if g == 2:
            whole(picked.at[0], incoming.at[0], 0).wait_send()
            send_panels(1)
        last = lax.fori_loop(g * turns, (g + 1) * turns, tiles, last)

    last = list(last)
    sources = [lax.rem(col + nc - d, nc) for d in range(nc)]
    before = [link(last, tg[sources[d]], slots + d) for d in range(nc)]
    sim_copy.wait()
    parts[slots] = parts[before[0]] + jnp.dot(
        sim[sources[0]], items[sl[col]], preferred_element_type=F32
    )

    def finish(h, grad):
        cut = slice(h * half, (h + 1) * half)
        whole(picked.at[h], incoming.at[h], h).wait_recv()
        for d in range(1, nc):
            part = jnp.dot(sim[sources[d]], incoming[h, d - 1], preferred_element_type=F32)
            parts[slots + d, :, cut] = part + parts[before[d], :, cut]
        top = jnp.zeros((8, half), F32)
        for i in range(ntiles):
            value = parts[last[i], :, cut]
            top = jnp.maximum(top, jnp.max(jnp.abs(value).reshape(tile // 8, 8, half), axis=0))
            for j in range(tile // chunk):
                n = i * (tile // chunk) + j
                grad[n // nz, n % nz] = value[j * chunk:(j + 1) * chunk]
        return step_of(top)

    def step_of(top):
        top = jnp.max(jnp.max(top, axis=0, keepdims=True), axis=1, keepdims=True)
        return jnp.maximum(top, 1e-20) / LEVELS

    def code(value, inverse):
        return jnp.round(value * inverse).astype(jnp.int32).astype(I16)

    step = finish(0, grad_a)
    steps[0] = jnp.broadcast_to(step, (1, half))
    inverse = 1.0 / step
    for d in z_order:
        other, device = along_z[d]
        push(steps.at[0], step_a.at[d - 1], 7, device)
        send_a[d - 1] = code(grad_a[:, other], inverse)
        push(send_a.at[d - 1], recv_a.at[d - 1], 2, device)
    step = finish(1, grad_b)
    steps[1] = jnp.broadcast_to(step, (1, half))
    inverse = 1.0 / step
    for d in y_order:
        other, device = along_y[d]
        push(steps.at[1], step_b.at[d - 1], 8, device)
        send_b[d - 1] = code(grad_b[other], inverse)
        push(send_b.at[d - 1], recv_b.at[d - 1], 3, device)

    whole(step_b, step_b, 8).wait_recv()
    whole(send_b, recv_b, 3).wait_recv()
    total = grad_b[y]
    for d in range(ny - 1):
        total = total + recv_b[d].astype(F32) * step_b[d]
    acc_b[...] = total
    step = step_of(jnp.max(jnp.abs(total).reshape(-1, 8, half), axis=0))
    steps[2] = jnp.broadcast_to(step, (1, half))
    send2_b[...] = code(total, 1.0 / step)
    for d in z_order:
        push(steps.at[2], step2_b.at[d - 1], 9, along_z[d][1])
        push(send2_b.at[along_z[d][0]], recv2_b.at[d - 1], 4, along_z[d][1])

    whole(step_a, step_a, 7).wait_recv()
    whole(send_a, recv_a, 2).wait_recv()
    total = grad_a[:, z]
    for d in range(nz - 1):
        total = total + recv_a[d].astype(F32) * step_a[d]
    acc_a[...] = total
    step = step_of(jnp.max(jnp.abs(total).reshape(-1, 8, half), axis=0))
    steps[3] = jnp.broadcast_to(step, (1, half))
    send2_a[...] = code(total, 1.0 / step)
    for d in y_order:
        push(steps.at[3], step2_a.at[d - 1], 11, along_y[d][1])
        push(send2_a.at[along_y[d][0]], recv2_a.at[d - 1], 10, along_y[d][1])

    whole(step2_b, step2_b, 9).wait_recv()
    whole(send2_b.at[pl.ds(0, nz - 1)], recv2_b, 4).wait_recv()
    own_b = acc_b[z]
    for d in range(nz - 1):
        own_b = own_b + recv2_b[d].astype(F32) * step2_b[d]
    whole(step2_a, step2_a, 11).wait_recv()
    whole(send2_a.at[pl.ds(0, ny - 1)], recv2_a, 10).wait_recv()
    own_a = acc_a[y]
    for d in range(ny - 1):
        own_a = own_a + recv2_a[d].astype(F32) * step2_a[d]

    part = jnp.sum(own_a * own_a + own_b * own_b, axis=0, keepdims=True)
    for n, (ring, recv) in enumerate(((first_ring, recv_p), (second_ring, recv_q))):
        squares[n] = part
        for d, device in enumerate(ring):
            push(squares.at[n], recv.at[d], 5 + n, device)
        whole(recv, recv, 5 + n).wait_recv()
        part = part + jnp.sum(recv[...], axis=0)
    entries = nc * ny * nz * chunk * rank
    root = jnp.sqrt(jnp.sum(part, axis=1, keepdims=True) / entries + 1e-06)

    mine_copy.wait()
    mixed = mine[...].astype(F32)
    out[:, :half] = mixed[:, :half] - 0.5 * own_a / root
    out[:, half:] = mixed[:, half:] - 0.5 * own_b / root

    whole(picked.at[1], incoming.at[1], 1).wait_send()
    whole(send_a, recv_a, 2).wait_send()
    whole(send_b, recv_b, 3).wait_send()
    whole(send2_b.at[pl.ds(0, nz - 1)], recv2_b, 4).wait_send()
    whole(send2_a.at[pl.ds(0, ny - 1)], recv2_a, 10).wait_send()
    whole(step2_a, step2_a, 11).wait_send()
    whole(recv_p, recv_p, 5).wait_send()
    whole(recv_q, recv_q, 6).wait_send()
    whole(step_a, step_a, 7).wait_send()
    whole(step_b, step_b, 8).wait_send()
    whole(step2_b, step2_b, 9).wait_send()


def shards(
    users, items, ratings, tile_users, tile_items, tile_count, send_list, block_target, similarity
):
    icount, rank = items.shape[1:]
    tile = ratings.shape[-1]
    slots = ratings.shape[2]
    ntiles = icount // tile
    utiles = users.shape[0] // tile
    nrows = lax.axis_size("rows")
    nc = lax.axis_size("cols")
    nz, ny, nx = NZ, nrows // NZ, nc // CORES
    chunk = icount // nrows
    half = rank // 2
    hbm = pl.BlockSpec(memory_space=pltpu.HBM)

    updated = pl.pallas_call(
        functools.partial(kernel, ny, nz, nx),
        out_shape=jax.ShapeDtypeStruct((chunk, rank), F32),
        in_specs=[pl.BlockSpec(memory_space=pltpu.SMEM)] + [hbm] * 9,
        out_specs=pl.BlockSpec(memory_space=VMEM),
        scratch_shapes=[
            pltpu.SMEM((slots,), jnp.int32),
            pltpu.SMEM((slots,), jnp.int32),
            pltpu.SMEM((nc,), jnp.int32),
            pltpu.SMEM((nc,), jnp.int32),
            VMEM((utiles, tile, rank), BF16),
            VMEM((ntiles, tile, rank), BF16),
            VMEM((slots, tile, tile), BF16),
            VMEM((nc, tile, tile), BF16),
            VMEM((chunk, rank), BF16),
            VMEM((utiles, rank, tile), BF16),
            VMEM((2, nc - 1, tile, half), BF16),
            VMEM((2, nc - 1, tile, half), BF16),
            VMEM((slots + nc + 1, tile, rank), F32),
            VMEM((ny, nz, chunk, half), F32),
            VMEM((ny, nz, chunk, half), F32),
            VMEM((nz - 1, ny, chunk, half), I16),
            VMEM((ny - 1, nz, chunk, half), I16),
            VMEM((nz - 1, ny, chunk, half), I16),
            VMEM((ny - 1, nz, chunk, half), I16),
            VMEM((ny, chunk, half), F32),
            VMEM((nz, chunk, half), F32),
            VMEM((ny, chunk, half), I16),
            VMEM((nz, chunk, half), I16),
            VMEM((ny - 1, chunk, half), I16),
            VMEM((nz - 1, chunk, half), I16),
            VMEM((2, 1, half), F32),
            VMEM((nz * CORES - 1, 1, half), F32),
            VMEM((ny * nx - 1, 1, half), F32),
            VMEM((4, 1, half), F32),
            VMEM((nz - 1, 1, half), F32),
            VMEM((ny - 1, 1, half), F32),
            VMEM((ny - 1, 1, half), F32),
            VMEM((nz - 1, 1, half), F32),
            pltpu.SemaphoreType.DMA((12,)),
            pltpu.SemaphoreType.DMA((12,)),
            pltpu.SemaphoreType.DMA((12,)),
        ],
        compiler_params=pltpu.CompilerParams(
            collective_id=0, has_side_effects=True, vmem_limit_bytes=40 << 20
        ),
        name="item_update",
    )(
        tile_count[0],
        *(
            pltpu.with_memory_space_constraint(a, pltpu.HBM)
            for a in (
                tile_users[0, 0], tile_items[0, 0], send_list[0, 0].reshape(-1), block_target[0, 0],
                users.reshape(-1, tile, rank), items[0].reshape(-1, tile, rank),
                ratings[0, 0], similarity[0, 0], items[0].reshape(nrows, chunk, rank),
            )
        ),
    )
    return updated[None]


def solution(mesh):
    in_specs = (
        P("rows", None),
        P("cols", None, None),
        P("rows", "cols", None, None, None),
        P("rows", "cols", None),
        P("rows", "cols", None),
        P("rows", "cols"),
        P("rows", "cols", None, None),
        P("rows", "cols", None),
        P("rows", "cols", None, None, None),
    )
    out_specs = P("cols", "rows", None)
    return jax.shard_map(shards, mesh=mesh, in_specs=in_specs, out_specs=out_specs, check_vma=False)
```
